32 devices in a mesh: section: 8 (over z, x), tensor: 4 (over y, core).
Axes of the slice: x: 2, y: 2, z: 4, core: 2. Of those that a mesh axis runs over, the one named last changes fastest.
Arguments:
- noise: float32 [2, 4, 8, 32], P(None, None, 'tensor'), may hold values from -6 to 6
- target: float32 [2, 4, 8, 32], P(None, None, 'tensor'), may hold values from -6 to 6
- timesteps: int32 [8], replicated, may hold values from 1 to 160, as said below
- w_in: float32 [4, 320], replicated, may hold values from -3 to 3
- gn_gain: float32 [320], replicated, may hold values from 0.1 to 1.9
- w_time1: float32 [320, 1280], replicated, may hold values from -0.3125 to 0.3125
- w_time2: float32 [1280, 320], replicated, may hold values from -0.15625 to 0.15625
- w_conv: bfloat16 [9, 320, 320], replicated, may hold values from -0.109375 to 0.109375
- w_out: float32 [320, 4], replicated, may hold values from -0.3125 to 0.3125
Outputs:
- trajectory: float32 [8, 2, 4, 8, 32], P('section', None, None, 'tensor')
- grad_conv: float32 [9, 320, 320], P(None, None, 'tensor')
The draws below stay inside these ranges and needn't reach their ends.
Inputs may be any that keep to these rules, and one draw needn't show every extreme that they name: `timesteps`: 8 distinct plan indices, strictly falling from one step to the next.
All inputs are finite; a program needn't handle non-finite values.
Results may differ from the reference program's by a relative error of at most 0.0008.
Values sent between devices are 32-bit elements; how exact they have to be, the bound alone decides.
A program may use at most 64 MiB of HBM per device.

```python
import math
import jax
import jax.numpy as jnp
from jax import lax

C = 320
TEMB = 1280
GROUPS = 32
CHAN_IN = 4
WIDTH = 32
MICRO = 2
STEPS = 8
H = 8


def draw_timesteps(key, part):
    picked = jax.random.permutation(key, 20 * STEPS)[:STEPS] + 1
    return (-jnp.sort(-picked)).astype(jnp.int32)


def shard_levels(own_key, dims, shards, low, largest):
    gain, own = 1.0, jax.random.fold_in(own_key, 6)
    for position, parts in shards:
        heights = jnp.exp(jax.random.uniform(jax.random.fold_in(own, position), (parts,), jnp.float32, low / len(shards), largest / len(shards)))
        gain = gain * jnp.repeat(heights, dims[position] // parts).reshape([-1 if axis == position else 1 for axis in range(len(dims))])
    return gain


def centred(own_key, extent, spread, limit, split=(), kind=jnp.bfloat16):
    result = jax.random.normal(own_key, extent, jnp.float32) * spread
    if len(split) > 0:
        result = shard_levels(own_key, extent, split, -0.22, 0.18) * result
    return jnp.clip(result, min=-limit, max=limit).astype(kind)


def setup_inputs(seed: int = 0) -> dict:
    arg_keys = jax.random.split(jax.random.key(seed), 10)
    return {
        "noise": centred(arg_keys[0], (MICRO, CHAN_IN, H, WIDTH), 1.0, 6.0, ((2, 4),), jnp.float32),
        "target": centred(arg_keys[1], (MICRO, CHAN_IN, H, WIDTH), 1.0, 6.0, ((2, 4),), jnp.float32),
        "timesteps": draw_timesteps(jax.random.fold_in(arg_keys[9], 71), 0),
        "w_in": centred(arg_keys[3], (CHAN_IN, C), CHAN_IN ** -0.5, 3.0, (), jnp.float32),
        "gn_gain": jnp.clip(1.0 + 0.18 * jax.random.normal(arg_keys[4], (C,), jnp.float32), 0.1, 1.9),
        "w_time1": centred(arg_keys[5], (C, TEMB), C ** -0.5, 0.3125, (), jnp.float32),
        "w_time2": centred(arg_keys[6], (TEMB, C), TEMB ** -0.5, 0.15625, (), jnp.float32),
        "w_conv": centred(arg_keys[7], (9, C, C), (9 * C) ** -0.5, 0.109375),
        "w_out": centred(arg_keys[8], (C, CHAN_IN), C ** -0.5, 0.3125, (), jnp.float32),
    }


precise = lax.Precision.HIGHEST

def alpha_table():
    step_grid = jnp.arange(1000, dtype=jnp.float32)
    lowest = jnp.sqrt(jnp.asarray(0.00085, jnp.float32))
    highest = jnp.sqrt(jnp.asarray(0.012, jnp.float32))
    betas = (lowest + step_grid * ((highest - lowest) / 999.0)) ** 2
    return jnp.cumprod(1.0 - betas)

def section_terms(timesteps, section_index, alphas, w_time1, w_time2, features):
    positions = jnp.arange(timesteps.shape[0], dtype=jnp.int32)
    current = jnp.sum(jnp.where(positions == section_index, timesteps, 0))
    following = jnp.sum(jnp.where(positions == section_index + 1, timesteps, 0))
    step_grid = jnp.arange(alphas.shape[0], dtype=jnp.int32)
    alpha_now = jnp.sum(jnp.where(step_grid == current, alphas, 0.0))
    alpha_next = jnp.where(section_index + 1 < timesteps.shape[0], jnp.sum(jnp.where(step_grid == following, alphas, 0.0)), 1.0)
    keep_coef = jnp.sqrt(alpha_next / alpha_now)
    noise_coef = jnp.sqrt(1.0 - alpha_next) - keep_coef * jnp.sqrt(1.0 - alpha_now)
    half_width = features // 2
    frequency = jnp.exp(-math.log(10000.0) * jnp.arange(half_width, dtype=jnp.float32) / half_width)
    angles = current.astype(jnp.float32) * frequency
    sinusoid = jnp.concatenate([jnp.cos(angles), jnp.sin(angles)])
    hidden = jax.nn.silu(jnp.dot(sinusoid, w_time1, precision=precise))
    return (keep_coef, noise_coef, jnp.dot(hidden, w_time2, precision=precise))

def group_partial(latent, w_in, groups):
    projected = jnp.einsum('crw,cd->rwd', latent, w_in, precision=precise)
    grouped = projected.reshape(-1, groups, projected.shape[2] // groups)
    return (lax.optimization_barrier(jnp.sum(grouped, axis=(0, 2))), lax.optimization_barrier(jnp.sum(grouped * grouped, axis=(0, 2))))

def denoise_rows(latent_pad, row_mask, group_sum, squares, w_in, gn_gain, conv_weight, w_out, embed, keep_coef, noise_coef, count_all):
    projected = jnp.einsum('crw,cd->rwd', latent_pad, w_in, precision=precise)
    groups = group_sum.shape[0]
    features = projected.shape[2]
    group_avg = group_sum / count_all
    group_var = squares / count_all - group_avg * group_avg
    average = jnp.repeat(group_avg, features // groups)
    variance = jnp.repeat(group_var, features // groups)
    activated = jax.nn.silu((projected - average) * lax.rsqrt(variance + 1e-05) * gn_gain) * row_mask[:, None, None]
    activated = activated + lax.stop_gradient(activated.astype(jnp.bfloat16).astype(jnp.float32) - activated)
    activated = jnp.pad(activated, ((0, 0), (1, 1), (0, 0)))
    row_count = latent_pad.shape[1] - 2
    col_count = latent_pad.shape[2]
    convolved = jnp.zeros((row_count, col_count, features), jnp.float32)
    for offset in range(9):
        shift_row = offset // 3
        shift_col = offset % 3
        window = activated[shift_row:shift_row + row_count, shift_col:shift_col + col_count]
        convolved = convolved + jnp.einsum('rwc,cd->rwd', window, conv_weight[offset], precision=precise)
    hidden = projected[1:-1] + convolved + embed
    guess = jnp.einsum('rwd,dc->crw', hidden, w_out, precision=precise)
    return keep_coef * latent_pad[:, 1:-1] + noise_coef * guess

def reference(noise, target, timesteps, w_in, gn_gain, w_time1, w_time2, w_conv, w_out):
    alphas = alpha_table()
    micro_count, channels, height, breadth = noise.shape
    features = w_in.shape[1]
    count_all = jnp.asarray(height * breadth * (features // GROUPS), jnp.float32)
    row_mask = jnp.pad(jnp.ones((height,), jnp.float32), 1)
    section_ids = jnp.arange(STEPS, dtype=jnp.int32)

    def run_chain(conv_weight):

        def advance(latent, section_index):
            keep_coef, noise_coef, embed = section_terms(timesteps, section_index, alphas, w_time1, w_time2, features)
            group_sum, squares = group_partial(latent, w_in, GROUPS)
            latent_pad = jnp.pad(latent, ((0, 0), (1, 1), (0, 0)))
            stepped = denoise_rows(latent_pad, row_mask, group_sum, squares, w_in, gn_gain, conv_weight, w_out, embed, keep_coef, noise_coef, count_all)
            return (stepped, stepped)
        trajectories = []
        for micro_index in range(micro_count):
            _, steps_out = lax.scan(advance, noise[micro_index], section_ids)
            trajectories.append(steps_out)
        return jnp.stack(trajectories, axis=1)
    trajectory, pullback = jax.vjp(run_chain, w_conv.astype(jnp.float32))
    cotangent = jnp.zeros_like(trajectory).at[STEPS - 1].set(trajectory[STEPS - 1] - target)
    grad_conv = pullback(cotangent)[0]
    return (trajectory, grad_conv)
```

```python
import functools
import math

import jax
import jax.numpy as jnp
import numpy as np
from jax import lax
from jax.experimental import pallas as pl
from jax.experimental.pallas import tpu as pltpu
from jax.sharding import PartitionSpec as P

GROUPS = 32
MESH = pl.DeviceIdType.MESH
HIGH = lax.Precision.HIGHEST
F32 = jnp.float32
BF16 = jnp.bfloat16
R = 8
LANES = 128


def alpha_table():
    step_grid = jnp.arange(1000, dtype=F32)
    lowest = jnp.sqrt(jnp.asarray(0.00085, F32))
    highest = jnp.sqrt(jnp.asarray(0.012, F32))
    betas = (lowest + step_grid * ((highest - lowest) / 999.0)) ** 2
    return jnp.cumprod(1.0 - betas)


def step_terms(timesteps, features):
    steps = timesteps.shape[0]
    table = alpha_table()
    grid = jnp.arange(table.shape[0], dtype=jnp.int32)
    now = jnp.sum(jnp.where(grid[None] == timesteps[:, None], table[None], 0.0), axis=1)
    after = jnp.concatenate([now[1:], jnp.ones((1,), F32)])
    keep = jnp.sqrt(after / now)
    noise = jnp.sqrt(1.0 - after) - keep * jnp.sqrt(1.0 - now)
    half = features // 2
    frequency = jnp.exp(-math.log(10000.0) * jnp.arange(half, dtype=F32) / half)
    angles = timesteps.astype(F32)[:, None] * frequency[None]
    return keep, noise, jnp.concatenate([jnp.cos(angles), jnp.sin(angles)], axis=1)


def parts3(x):
    high = x.astype(BF16).astype(F32)
    rest = x - high
    mid = rest.astype(BF16).astype(F32)
    low = (rest - mid).astype(BF16).astype(F32)
    return high, mid, low


def parts2(x):
    high = x.astype(BF16)
    return high, (x - high.astype(F32)).astype(BF16)


def iota(shape, axis):
    return lax.broadcasted_iota(jnp.int32, shape, axis)


def nn(a, b, precision=None):
    return lax.dot_general(a, b, (((1,), (0,)), ((), ())), precision=precision, preferred_element_type=F32)


def nt(a, b, precision=None):
    return lax.dot_general(a, b, (((1,), (1,)), ((), ())), precision=precision, preferred_element_type=F32)


def tn(a, b, precision=None):
    return lax.dot_general(a, b, (((0,), (0,)), ((), ())), precision=precision, preferred_element_type=F32)


def wide(column, lanes):
    return jnp.concatenate([column] * (lanes // LANES), axis=1) if lanes > LANES else column


def chain_kernel(dims, keep_ref, noise_ref, x_ref, sinus_ref, win_ref, gain_ref, wout_ref, w1_hbm, w2_hbm, wc_hbm,
                 path_ref, g_ref, w1, w2, wc, sems, act_s, z_s, scale_s, avg_s, rstd_s, wext, sm6, smt, v3, vt3, w2t, mask, ebs, gacc):
    height, width, features, steps, chans, taps_side = dims
    taps = taps_side * taps_side
    lanes = height * width
    count = float(lanes * (features // GROUPS))
    per_group = features // GROUPS
    blocks = 1 + chans
    qrows = blocks * R
    tcols = taps * R

    copies = [pltpu.make_async_copy(src, dst, sems.at[i]) for i, (src, dst) in enumerate(((wc_hbm, wc), (w1_hbm, w1), (w2_hbm, w2)))]
    for copy in copies:
        copy.start()

    lane = iota((R, lanes), 1)
    row, col = lane // width, lane % width
    offsets = []
    for tap in range(taps):
        dy, dx = tap // taps_side - taps_side // 2, tap % taps_side - taps_side // 2
        offsets.append(dy * width + dx)
        ok = (row + dy >= 0) & (row + dy < height) & (col + dx >= 0) & (col + dx < width)
        mask[tap * R:(tap + 1) * R] = ok.astype(F32)

    win = win_ref[...]
    wout = wout_ref[...]
    def picker(cols):
        return (iota((chans, cols), 1) % R == iota((chans, cols), 0)).astype(F32)
    win_t = tn(win, picker(6 * qrows), HIGH)
    wout_t = nn(wout, picker(3 * tcols), HIGH)
    gain_col = tn(gain_ref[...], jnp.ones((1, LANES), F32), HIGH)
    woutT = jnp.transpose(wout_t[:, :LANES])[:R]
    win8 = jnp.concatenate([win, jnp.zeros((R - chans, features), F32)], axis=0) if chans < R else win

    pa, pb, pc = parts3(jnp.concatenate([win_t[:, :6 * R], nn(woutT, win_t[:, :6 * R], HIGH)], axis=0))
    blk = iota(pa.shape, 1) // R
    wext[...] = jnp.where((blk == 2) | (blk == 4), pb, jnp.where(blk == 5, pc, pa)).astype(BF16)

    qlane = iota(win_t.shape, 1)
    qblk = (qlane % qrows) // R
    prod = win_t
    for c in range(chans):
        prod = jnp.where(qblk == c + 1, win_t * win_t[:, c:c + 1], prod)
    member = (iota((features, features), 0) // per_group == iota((features, features), 1) // per_group).astype(BF16)
    sa, sb, sc = parts3(prod)
    sums = (nn(member, sa.astype(BF16)) + nn(member, sb.astype(BF16)) + nn(member, sc.astype(BF16))) * (1.0 / count)
    sa, sb, sc = parts3(sums)
    rep = qlane // qrows
    chosen = jnp.where((rep == 2) | (rep == 4), sb, jnp.where(rep == 5, sc, sa))
    sm6[:features] = jnp.where(qblk == 0, chosen, 0.0).astype(BF16)
    sm6[features:] = jnp.where(qblk == 0, 0.0, chosen).astype(BF16)
    pad = 2 * LANES if qrows > LANES else LANES
    sumsT = jnp.transpose(sums[:, :pad])[:qrows]
    th, tm = parts2(sumsT)
    smt[:qrows] = th
    smt[qrows:] = tm
    wh, wm = parts2(jnp.concatenate([win8, jnp.zeros((R, features), F32)], axis=0))
    w2t[:2 * R] = wh
    w2t[2 * R:] = wm

    copies[0].wait()
    oa, ob, oc = parts3(wout_t)
    tblk = iota(wout_t.shape, 1) // R % taps
    v = jnp.zeros((features, 3 * tcols), F32)
    for tap in range(taps):
        weights = wc[tap]
        for part in (oa, ob, oc):
            v = v + nn(weights, jnp.where(tblk == tap, part, 0.0).astype(BF16))
    both = nn(win8, wout_t, HIGH)
    both = jnp.where(iota(both.shape, 1) // R % taps == taps // 2, both, 0.0)
    v_all = jnp.concatenate([v, both], axis=0)
    va, vb, _ = parts3(v_all)
    third = iota(v_all.shape, 1) // tcols
    v3[...] = jnp.where(third == 1, vb, va).astype(BF16)
    cols = -(-3 * tcols // LANES) * LANES
    v_pad = jnp.concatenate([v, jnp.zeros((features, cols - 3 * tcols), F32)], axis=1) if cols > 3 * tcols else v
    vT = jnp.transpose(v_pad)[:3 * tcols]
    va, vb, vc = parts3(vT)
    third = iota(vT.shape, 0) // tcols
    vt3[...] = jnp.where(third == 1, vb, jnp.where(third == 2, vc, va)).astype(BF16)

    copies[1].wait()
    copies[2].wait()
    hidden = nn(sinus_ref[...], w1[...], HIGH)
    hidden = hidden * (1.0 / (1.0 + jnp.exp(-hidden)))
    embed = nn(hidden, w2[...], HIGH)
    embed_out = nt(woutT, embed, HIGH)
    for s in range(steps):
        ebs[s] = jnp.broadcast_to(embed_out[:, s:s + 1], (R, LANES))

    start = x_ref[0]
    target = x_ref[1]
    for n in range(2, x_ref.shape[0], 2):
        start = start + x_ref[n]
        target = target + x_ref[n + 1]

    def forward(s, x):
        xa, xb, xc = parts3(x)
        x6 = jnp.concatenate([xa, xb, xa, xc, xb, xa], axis=0).astype(BF16)
        projected = nn(wext[...], x6)
        q = jnp.concatenate([x] + [x * x[c:c + 1] for c in range(chans)], axis=0)
        qs = jnp.broadcast_to(jnp.sum(q, axis=1, keepdims=True), (qrows, LANES))
        qa, qb, qc = parts3(qs)
        q6 = jnp.concatenate([qa, qb, qa, qc, qb, qa], axis=0).astype(BF16)
        stats = nn(sm6[...], q6)
        average = stats[:features]
        variance = stats[features:] - average * average
        rstd = lax.rsqrt(variance + 1e-05)
        scale = rstd * gain_col
        avg_s[s] = average
        rstd_s[s] = rstd
        scale_s[s] = scale
        z = (projected[:features] - wide(average, lanes)) * wide(scale, lanes)
        z_s[s] = z
        act = (z * (0.5 * jnp.tanh(0.5 * z) + 0.5)).astype(BF16)
        act_s[s] = act
        y = nn(vt3[...], act)
        y = y[:tcols] + (y[tcols:2 * tcols] + y[2 * tcols:])
        guess = projected[features:] + wide(ebs[s], lanes)
        for tap in range(taps):
            piece = y[tap * R:(tap + 1) * R]
            if offsets[tap] % lanes:
                piece = pltpu.roll(piece, (-offsets[tap]) % lanes, 1) * mask[tap * R:(tap + 1) * R]
            guess = guess + piece
        x = keep_ref[s] * x + noise_ref[s] * guess
        path_ref[s + 1] = x
        return x

    path_ref[0] = start
    last = lax.fori_loop(0, steps, forward, start)
    gacc[...] = jnp.zeros_like(gacc)

    def backward(i, adjoint):
        s = steps - 1 - i
        a = noise_ref[s] * adjoint
        shifted = []
        for tap in range(taps):
            piece = a
            if offsets[tap] % lanes:
                piece = pltpu.roll(a * mask[tap * R:(tap + 1) * R], offsets[tap] % lanes, 1)
            shifted.append(piece)
        shifted = jnp.concatenate(shifted, axis=0)
        high = shifted.astype(BF16).astype(F32)
        low = shifted - high
        a3 = jnp.concatenate([high, high, low], axis=0).astype(BF16)
        grads = nn(v3[...], a3)
        gacc[...] += nt(jnp.concatenate([high, low], axis=0).astype(BF16), act_s[s])
        z = z_s[s]
        sig = 0.5 * jnp.tanh(0.5 * z) + 0.5
        slope = sig + z * sig * (1.0 - sig)
        dz = grads[:features] * slope
        dzs = dz * wide(scale_s[s], lanes)
        rstd = rstd_s[s]
        e1 = jnp.broadcast_to(jnp.sum(dzs, axis=1, keepdims=True), (features, LANES))
        e2 = jnp.broadcast_to(jnp.sum(dz * z, axis=1, keepdims=True), (features, LANES)) * (rstd * rstd)
        pair = jnp.concatenate([e2 * avg_s[s] - e1, e2], axis=1)
        ph, pm = parts2(pair)
        k = nn(smt[...], ph)
        k = k[:qrows] + k[qrows:] + nn(smt[:qrows], pm)
        dh, dm = parts2(dzs)
        direct = nn(w2t[...], dh)
        direct = direct[:R] + direct[2 * R:3 * R] + nn(w2t[:2 * R], dm)[:R]
        result = keep_ref[s] * adjoint + grads[features:] + direct + wide(k[:R, :LANES], lanes)
        x = path_ref[s]
        for c in range(chans):
            result = result - wide(k[(c + 1) * R:(c + 2) * R, LANES:], lanes) * x[c:c + 1]
        return result

    lax.fori_loop(0, steps, backward, last - target)
    g_ref[...] = gacc[:tcols] + gacc[tcols:]


def run_chain(x, keep, noise_coef, sinus, w_in, gn_gain, w_time1, w_time2, w_conv, w_out, height, width):
    chans, features = w_in.shape
    steps = keep.shape[0]
    temb = w_time1.shape[1]
    taps = w_conv.shape[0]
    side = math.isqrt(taps)
    lanes = height * width
    qrows = (1 + chans) * R
    tcols = taps * R
    vmem = pl.BlockSpec(memory_space=pltpu.VMEM)
    smem = pl.BlockSpec(memory_space=pltpu.SMEM)
    hbm = pl.BlockSpec(memory_space=pl.ANY)
    return pl.pallas_call(
        functools.partial(chain_kernel, (height, width, features, steps, chans, side)),
        out_shape=(jax.ShapeDtypeStruct((steps + 1, R, lanes), F32), jax.ShapeDtypeStruct((tcols, features), F32)),
        in_specs=[smem, smem, vmem, vmem, vmem, vmem, vmem, hbm, hbm, hbm],
        out_specs=(vmem, vmem),
        scratch_shapes=[
            pltpu.VMEM((features, temb), F32),
            pltpu.VMEM((temb, features), F32),
            pltpu.VMEM((taps, features, features), BF16),
            pltpu.SemaphoreType.DMA((3,)),
            pltpu.VMEM((steps, features, lanes), BF16),
            pltpu.VMEM((steps, features, lanes), F32),
            pltpu.VMEM((steps, features, LANES), F32),
            pltpu.VMEM((steps, features, LANES), F32),
            pltpu.VMEM((steps, features, LANES), F32),
            pltpu.VMEM((features + R, 6 * R), BF16),
            pltpu.VMEM((2 * features, 6 * qrows), BF16),
            pltpu.VMEM((2 * qrows, features), BF16),
            pltpu.VMEM((features + R, 3 * tcols), BF16),
            pltpu.VMEM((3 * tcols, features), BF16),
            pltpu.VMEM((4 * R, features), BF16),
            pltpu.VMEM((tcols, lanes), F32),
            pltpu.VMEM((steps, R, LANES), F32),
            pltpu.VMEM((2 * tcols, features), F32),
        ],
        compiler_params=pltpu.CompilerParams(vmem_limit_bytes=60 * 1024 * 1024),
        name="chain",
    )(keep, noise_coef, x, sinus, w_in, gn_gain.reshape(1, features), w_out, w_time1, w_time2, w_conv)


def barrier_with(peers):
    barrier = pltpu.get_barrier_semaphore()
    for peer in peers:
        pl.semaphore_signal(barrier, inc=1, device_id={"tensor": peer}, device_id_type=MESH)
    pl.semaphore_wait(barrier, len(peers))


def gather_kernel(size, micro, mine_ref, slots_ref, send, recv, own):
    me = lax.axis_index("tensor")
    peers = [lax.rem(me + d, size) for d in range(1, size)]
    barrier_with(peers)
    copies = []
    for d, peer in enumerate(peers):
        copies.append(pltpu.make_async_remote_copy(
            src_ref=mine_ref.at[lax.rem(peer, micro)], dst_ref=slots_ref.at[d + 1],
            send_sem=send.at[d], recv_sem=recv.at[d], device_id={"tensor": peer}, device_id_type=MESH))
    for copy in copies:
        copy.start()
    local = pltpu.make_async_copy(mine_ref.at[lax.rem(me, micro)], slots_ref.at[0], own)
    local.start()
    local.wait()
    for copy in copies:
        copy.wait()


def gather(mine, size, micro):
    vmem = pl.BlockSpec(memory_space=pltpu.VMEM)
    return pl.pallas_call(
        functools.partial(gather_kernel, size, micro),
        out_shape=jax.ShapeDtypeStruct((size,) + mine.shape[1:], F32),
        in_specs=[vmem],
        out_specs=vmem,
        scratch_shapes=[pltpu.SemaphoreType.DMA((size - 1,)), pltpu.SemaphoreType.DMA((size - 1,)), pltpu.SemaphoreType.DMA],
        compiler_params=pltpu.CompilerParams(collective_id=0, has_side_effects=True),
        name="gather",
    )(mine)


def swap_kernel(micro, path_ref, g_ref, paths_ref, gs_ref, send, recv, own):
    section = lax.axis_index("section")
    me = lax.axis_index("tensor")
    mine = lax.rem(me, micro)
    peers = [me - mine + lax.rem(mine + d, micro) for d in range(1, micro)]
    barrier_with(peers)
    copies = []
    for d, peer in enumerate(peers):
        for k, (src, dst) in enumerate(((path_ref.at[section + 1], paths_ref.at[mine]), (g_ref, gs_ref.at[mine]))):
            copies.append(pltpu.make_async_remote_copy(
                src_ref=src, dst_ref=dst, send_sem=send.at[d, k], recv_sem=recv.at[d, k],
                device_id={"tensor": peer}, device_id_type=MESH))
    for copy in copies:
        copy.start()
    first = pltpu.make_async_copy(path_ref.at[section + 1], paths_ref.at[mine], own.at[0])
    second = pltpu.make_async_copy(g_ref, gs_ref.at[mine], own.at[1])
    first.start()
    second.start()
    first.wait()
    second.wait()
    for copy in copies:
        copy.wait()


def swap(path, g, micro):
    vmem = pl.BlockSpec(memory_space=pltpu.VMEM)
    return pl.pallas_call(
        functools.partial(swap_kernel, micro),
        out_shape=(jax.ShapeDtypeStruct((micro,) + path.shape[1:], F32), jax.ShapeDtypeStruct((micro,) + g.shape, F32)),
        in_specs=[vmem, vmem],
        out_specs=(vmem, vmem),
        scratch_shapes=[pltpu.SemaphoreType.DMA((micro - 1, 2)), pltpu.SemaphoreType.DMA((micro - 1, 2)), pltpu.SemaphoreType.DMA((2,))],
        compiler_params=pltpu.CompilerParams(collective_id=1, has_side_effects=True),
        name="swap",
    )(path, g)


def local(noise, target, timesteps, w_in, gn_gain, w_time1, w_time2, w_conv, w_out):
    size = lax.axis_size("tensor")
    me = lax.axis_index("tensor")
    micro, chans, rows, width = noise.shape
    features = w_in.shape[1]
    taps = w_conv.shape[0]
    height = rows * size
    span = rows * width
    lanes = height * width
    keep, noise_coef, sinus = step_terms(timesteps, features)

    flat = jnp.stack([noise.reshape(micro, chans, span), target.reshape(micro, chans, span)], axis=1)
    flat = jnp.pad(flat, ((0, 0), (0, 0), (0, R - chans), (0, 0)))
    here = jnp.arange(lanes, dtype=jnp.int32)[None, None, None] // span == me
    placed = jnp.where(here, jnp.tile(flat, (1, 1, 1, size)), 0.0)
    slots = gather(placed, size, micro)
    x = slots.reshape(2 * size, R, lanes)
    path, g = run_chain(x, keep, noise_coef, sinus, w_in, gn_gain, w_time1, w_time2, w_conv, w_out, height, width)
    paths, gs = swap(path, g, micro)
    out_path = lax.dynamic_slice(paths, (0, 0, me * span), (micro, chans, span)).reshape(1, micro, chans, rows, width)
    total = jnp.sum(gs, axis=0).reshape(taps, R, features)[:, :chans]
    share = features // size
    w_share = lax.dynamic_slice(w_out, (me * share, 0), (share, chans))
    grad = jnp.einsum("kcd,ec->kde", total, w_share, precision=HIGH)
    return out_path, grad


def solution(mesh):
    placed = (P(None, None, "tensor", None), P(None, None, "tensor", None)) + (P(),) * 7
    return jax.shard_map(
        local,
        mesh=mesh,
        in_specs=placed,
        out_specs=(P("section", None, None, "tensor", None), P(None, None, "tensor")),
        check_vma=False,
    )
```

```python
import functools
import math

import jax
import jax.numpy as jnp
from jax import lax
from jax.experimental import pallas as pl
from jax.experimental.pallas import tpu as pltpu
from jax.sharding import PartitionSpec as P

GROUPS = 32
MESH = pl.DeviceIdType.MESH
HIGH = lax.Precision.HIGHEST
F32 = jnp.float32
BF16 = jnp.bfloat16
R = 8
LANES = 128


def parts3(x):
    high = x.astype(BF16).astype(F32)
    rest = x - high
    mid = rest.astype(BF16).astype(F32)
    low = (rest - mid).astype(BF16).astype(F32)
    return high, mid, low


def parts2(x):
    high = x.astype(BF16)
    return high, (x - high.astype(F32)).astype(BF16)


def iota(shape, axis):
    return lax.broadcasted_iota(jnp.int32, shape, axis)


def nn(a, b, precision=None):
    return lax.dot_general(a, b, (((1,), (0,)), ((), ())), precision=precision, preferred_element_type=F32)


def nt(a, b, precision=None):
    return lax.dot_general(a, b, (((1,), (1,)), ((), ())), precision=precision, preferred_element_type=F32)


def tn(a, b, precision=None):
    return lax.dot_general(a, b, (((0,), (0,)), ((), ())), precision=precision, preferred_element_type=F32)


def wide(column, lanes):
    return jnp.concatenate([column] * (lanes // LANES), axis=1) if lanes > LANES else column


def dot3(a, b, dot):
    ah, am = parts2(a)
    bh, bm = parts2(b)
    return dot(ah, bh) + dot(am, bh) + dot(ah, bm)


def everywhere(value, combine):
    for axis in (1, 0):
        step = value.shape[axis] // 2
        while step:
            value = combine(value, pltpu.roll(value, step, axis))
            step //= 2
    return value


def step_coefficients(ts_ref, steps, keep_s, noise_s):
    index = iota((R, LANES), 0) * LANES + iota((R, LANES), 1)
    lowest = jnp.sqrt(jnp.full((R, LANES), 0.00085, F32))
    highest = jnp.sqrt(jnp.full((R, LANES), 0.012, F32))
    betas = (lowest + index.astype(F32) * ((highest - lowest) / 999.0)) ** 2
    factors = 1.0 - betas
    bars = [everywhere(jnp.where(index <= ts_ref[s], factors, 1.0), jnp.multiply) for s in range(steps)]
    bars.append(jnp.ones((R, LANES), F32))
    for s in range(steps):
        keep = jnp.sqrt(bars[s + 1] / bars[s])
        keep_s[s] = keep
        noise_s[s] = jnp.sqrt(1.0 - bars[s + 1]) - keep * jnp.sqrt(1.0 - bars[s])


def sinusoid(ts_ref, steps, features):
    half = features // 2
    shape = (steps, features)
    row, lane = iota(shape, 0), iota(shape, 1)
    times = jnp.zeros(shape, jnp.int32)
    for s in range(steps):
        times = jnp.where(row == s, ts_ref[s], times)
    place = jnp.where(lane < half, lane, lane - half).astype(F32)
    angles = times.astype(F32) * jnp.exp(-math.log(10000.0) * place / half)
    return jnp.where(lane < half, jnp.cos(angles), jnp.sin(angles))


def chain_kernel(dims, ts_ref, noise_ref, target_ref, win_ref, gain_ref, wout_ref, w1_hbm, w2_hbm, wc_hbm,
                 paths_ref, g_ref, w1, w2, wc, sems, mine, slots, send, recv, path, arrived, gsend, garrived, send2, recv2,
                 act_s, z_s, scale_s, avg_s, rstd_s, wext, sm6, smt, v3, vt3, w2t, mask, ebs, gacc, keep_s, noise_s):
    height, width, features, steps, chans, taps_side, size, micro = dims
    taps = taps_side * taps_side
    lanes = height * width
    rows = height // size
    span = rows * width
    per_group = features // GROUPS
    count = float(lanes * per_group)
    blocks = 1 + chans
    qrows = blocks * R
    tcols = taps * R
    section = lax.axis_index("section")
    me = lax.axis_index("tensor")
    own = lax.rem(me, micro)

    barrier = pltpu.get_barrier_semaphore()
    peers = [lax.rem(me + d, size) for d in range(1, size)]
    for peer in peers:
        pl.semaphore_signal(barrier, inc=1, device_id={"tensor": peer}, device_id_type=MESH)
    copies = [pltpu.make_async_copy(src, dst, sems.at[i]) for i, (src, dst) in enumerate(((wc_hbm, wc), (w1_hbm, w1), (w2_hbm, w2)))]
    for copy in copies:
        copy.start()
    mine[...] = jnp.zeros_like(mine)
    for m in range(micro):
        for r in range(rows):
            mine[m, :chans, r * width:(r + 1) * width] = noise_ref[m, :, r, :]
            mine[m, R:R + chans, r * width:(r + 1) * width] = target_ref[m, :, r, :]
    pl.semaphore_wait(barrier, size - 1)
    spread = [pltpu.make_async_remote_copy(
        src_ref=mine.at[lax.rem(peer, micro)], dst_ref=slots.at[d], send_sem=send.at[d], recv_sem=recv.at[d],
        device_id={"tensor": peer}, device_id_type=MESH) for d, peer in enumerate(peers)]
    for copy in spread:
        copy.start()

    step_coefficients(ts_ref, steps, keep_s, noise_s)

    lane = iota((R, lanes), 1)
    row, col = lane // width, lane % width
    offsets = []
    for tap in range(taps):
        dy, dx = tap // taps_side - taps_side // 2, tap % taps_side - taps_side // 2
        offsets.append(dy * width + dx)
        ok = (row + dy >= 0) & (row + dy < height) & (col + dx >= 0) & (col + dx < width)
        mask[tap * R:(tap + 1) * R] = ok.astype(F32)

    win, woutT = win_ref[...], wout_ref[...]
    if chans < R:
        fill = jnp.zeros((R - chans, features), F32)
        win, woutT = jnp.concatenate([win, fill], axis=0), jnp.concatenate([woutT, fill], axis=0)

    def tiled(weights, cols):
        high, mid, low = (part.astype(BF16) for part in parts3(weights))
        picker = (iota((R, cols), 1) % R == iota((R, cols), 0)).astype(BF16)
        return tn(high, picker) + tn(mid, picker) + tn(low, picker)

    win_t = tiled(win, 6 * qrows)
    wout_t = tiled(woutT, 3 * tcols)
    gain_row = gain_ref[...].reshape(1, features)
    gain_col = tn(gain_row, jnp.ones((1, LANES), F32), HIGH)

    pa, pb, pc = parts3(jnp.concatenate([win_t[:, :6 * R], dot3(woutT, win_t[:, :6 * R], nn)], axis=0))
    blk = iota(pa.shape, 1) // R
    wext[...] = jnp.where((blk == 2) | (blk == 4), pb, jnp.where(blk == 5, pc, pa)).astype(BF16)

    qlane = iota(win_t.shape, 1)
    qblk = (qlane % qrows) // R
    factor = jnp.ones_like(win_t)
    for c in range(chans):
        factor = jnp.where(qblk == c + 1, win_t[:, c:c + 1], factor)
    member = (iota((features, features), 0) // per_group == iota((features, features), 1) // per_group).astype(BF16)
    sa, sb = parts2(win_t * factor)
    sums = (nn(member, sa) + nn(member, sb)) * (1.0 / count)
    sa, sb, sc = parts3(sums)
    rep = qlane // qrows
    chosen = jnp.where((rep == 2) | (rep == 4), sb, jnp.where(rep == 5, sc, sa))
    sm6[:features] = jnp.where(qblk == 0, chosen, 0.0).astype(BF16)
    sm6[features:] = jnp.where(qblk == 0, 0.0, chosen).astype(BF16)
    pad = -(-qrows // LANES) * LANES
    th, tm = parts2(jnp.transpose(sums[:, :pad])[:qrows])
    smt[:qrows] = th
    smt[qrows:] = tm
    wh, wm = parts2(jnp.concatenate([win, jnp.zeros((R, features), F32)], axis=0))
    w2t[:2 * R] = wh
    w2t[2 * R:] = wm

    both = dot3(win, wout_t, nn)
    both = jnp.where(iota(both.shape, 1) // R % taps == taps // 2, both, 0.0)
    oh, om = parts2(wout_t)
    tblk = iota(wout_t.shape, 1) // R % taps
    sines = sinusoid(ts_ref, steps, features)
    copies[0].wait()
    v = jnp.zeros((features, 3 * tcols), F32)
    for start_tap in range(0, taps, taps_side):
        weights = wc[start_tap:start_tap + taps_side].reshape(taps_side * features, features)
        out = nn(weights, oh) + nn(weights, om)
        for i in range(taps_side):
            v = jnp.where(tblk == start_tap + i, out[i * features:(i + 1) * features], v)
    v_all = jnp.concatenate([v, both], axis=0)
    va, vb, _ = parts3(v_all)
    third = iota(v_all.shape, 1) // tcols
    v3[...] = jnp.where(third == 1, vb, va).astype(BF16)
    cols = -(-2 * tcols // LANES) * LANES
    vT = jnp.transpose(v[:, :cols] if cols <= 3 * tcols else jnp.concatenate([v, jnp.zeros((features, cols - 3 * tcols), F32)], axis=1))[:2 * tcols]
    va, vb, _ = parts3(vT)
    vt3[...] = jnp.where(iota(vT.shape, 0) // tcols == 1, vb, va).astype(BF16)

    copies[1].wait()
    hh, hm = parts2(sines)
    stacked = jnp.concatenate([hh.astype(F32), hm.astype(F32)], axis=0).astype(BF16)
    wh, wm = parts2(w1[...])
    first = nn(stacked, wh)
    hidden = first[:steps] + first[steps:] + nn(stacked, wm)[:steps]
    hidden = hidden * (0.5 * jnp.tanh(0.5 * hidden) + 0.5)
    copies[2].wait()
    hh, hm = parts2(hidden)
    stacked = jnp.concatenate([hh.astype(F32), hm.astype(F32)], axis=0).astype(BF16)
    wh, wm = parts2(w2[...])
    first = nt(wh, stacked)
    embed = first[:, :steps] + first[:, steps:] + nt(wm, stacked)[:, :steps]
    embed_out = dot3(woutT, embed, nn)
    for s in range(steps):
        ebs[s] = jnp.broadcast_to(embed_out[:, s:s + 1], (R, LANES))

    def unrolled(block, owner):
        if lanes > block.shape[1]:
            block = jnp.concatenate([block, jnp.zeros((2 * R, lanes - block.shape[1]), F32)], axis=1)
        return pltpu.roll(block, owner * span, 1)

    both = unrolled(mine[own], me)
    for d, copy in enumerate(spread):
        copy.wait()
        both = both + unrolled(slots[d], lax.rem(me + size - 1 - d, size))
    start, target = both[:R], both[R:]

    def forward(s, x):
        xa, xb, xc = parts3(x)
        x6 = jnp.concatenate([xa, xb, xa, xc, xb, xa], axis=0).astype(BF16)
        projected = nn(wext[...], x6)
        q = jnp.concatenate([x] + [x * x[c:c + 1] for c in range(chans)], axis=0)
        qs = jnp.broadcast_to(jnp.sum(q, axis=1, keepdims=True), (qrows, LANES))
        qa, qb, qc = parts3(qs)
        q6 = jnp.concatenate([qa, qb, qa, qc, qb, qa], axis=0).astype(BF16)
        stats = nn(sm6[...], q6)
        average = stats[:features]
        variance = stats[features:] - average * average
        rstd = lax.rsqrt(variance + 1e-05)
        scale = rstd * gain_col
        avg_s[s] = average
        rstd_s[s] = rstd
        scale_s[s] = scale
        z = (projected[:features] - wide(average, lanes)) * wide(scale, lanes)
        z_s[s] = z
        act = (z * (0.5 * jnp.tanh(0.5 * z) + 0.5)).astype(BF16)
        act_s[s] = act
        y = nn(vt3[...], act)
        y = y[:tcols] + y[tcols:]
        guess = projected[features:] + wide(ebs[s], lanes)
        for tap in range(taps):
            piece = y[tap * R:(tap + 1) * R]
            if offsets[tap] % lanes:
                piece = pltpu.roll(piece, (-offsets[tap]) % lanes, 1) * mask[tap * R:(tap + 1) * R]
            guess = guess + piece
        x = wide(keep_s[s], lanes) * x + wide(noise_s[s], lanes) * guess
        path[s + 1] = x
        return x

    path[0] = start
    last = lax.fori_loop(0, steps, forward, start)
    gacc[...] = jnp.zeros_like(gacc)

    def backward(i, adjoint):
        s = steps - 1 - i
        a = wide(noise_s[s], lanes) * adjoint
        shifted = []
        for tap in range(taps):
            piece = a
            if offsets[tap] % lanes:
                piece = pltpu.roll(a * mask[tap * R:(tap + 1) * R], offsets[tap] % lanes, 1)
            shifted.append(piece)
        shifted = jnp.concatenate(shifted, axis=0)
        high = shifted.astype(BF16).astype(F32)
        low = shifted - high
        a3 = jnp.concatenate([high, high, low], axis=0).astype(BF16)
        grads = nn(v3[...], a3)
        gacc[...] += nt(jnp.concatenate([high, low], axis=0).astype(BF16), act_s[s])
        z = z_s[s]
        sig = 0.5 * jnp.tanh(0.5 * z) + 0.5
        slope = sig + z * sig * (1.0 - sig)
        dz = grads[:features] * slope
        dzs = dz * wide(scale_s[s], lanes)
        rstd = rstd_s[s]
        e1 = jnp.broadcast_to(jnp.sum(dzs, axis=1, keepdims=True), (features, LANES))
        e2 = jnp.broadcast_to(jnp.sum(dz * z, axis=1, keepdims=True), (features, LANES)) * (rstd * rstd)
        pair = jnp.concatenate([e2 * avg_s[s] - e1, e2], axis=1)
        ph, pm = parts2(pair)
        k = nn(smt[...], ph)
        k = k[:qrows] + k[qrows:] + nn(smt[:qrows], pm)
        dh, dm = parts2(dzs)
        direct = nn(w2t[...], dh)
        direct = direct[:R] + direct[2 * R:3 * R] + nn(w2t[:2 * R], dm)[:R]
        result = wide(keep_s[s], lanes) * adjoint + grads[features:] + direct + wide(k[:R, :LANES], lanes)
        x = path[s]
        for c in range(chans):
            result = result - wide(k[(c + 1) * R:(c + 2) * R, LANES:], lanes) * x[c:c + 1]
        return result

    lax.fori_loop(0, steps, backward, last - target)
    garrived_total = gacc[:tcols] + gacc[tcols:]
    gsend[...] = garrived_total
    partners = [me - own + lax.rem(own + d, micro) for d in range(1, micro)]
    swaps = []
    for d, partner in enumerate(partners):
        for k, (src, dst) in enumerate(((path.at[section + 1], arrived.at[d]), (gsend, garrived.at[d]))):
            swaps.append(pltpu.make_async_remote_copy(
                src_ref=src, dst_ref=dst, send_sem=send2.at[d, k], recv_sem=recv2.at[d, k],
                device_id={"tensor": partner}, device_id_type=MESH))
    for copy in swaps:
        copy.start()
    paths_ref[own] = path[section + 1]
    for copy in swaps:
        copy.wait()
    total = garrived_total
    for d in range(micro - 1):
        total = total + garrived[d]
        paths_ref[lax.rem(own + micro - 1 - d, micro)] = arrived[d]
    g_ref[...] = total


def finish_kernel(dims, paths_ref, g_ref, wout_ref, traj_ref, grad_hbm, grads, sems):
    size, taps, span = dims
    me = lax.axis_index("tensor")
    _, micro, chans, rows, width = traj_ref.shape
    share = grads.shape[1]
    features = g_ref.shape[1]
    padded = -(-features // LANES) * LANES
    weights = jnp.concatenate([wout_ref[...], jnp.zeros((chans, padded - features), F32)], axis=1)
    weights = pltpu.roll(weights, lax.rem(padded - me * share, padded), 1)[:, :share]
    weights = jnp.concatenate([weights, jnp.zeros((R - chans, share), F32)], axis=0) if chans < R else weights
    wa, wb, _ = parts3(weights)
    left = jnp.concatenate([wa, wb, wa, wb], axis=0).astype(BF16)
    copies = []
    for tap in range(taps):
        ga, gb, _ = parts3(g_ref[tap * R:(tap + 1) * R])
        grads[tap] = tn(left, jnp.concatenate([ga, ga, gb, gb], axis=0).astype(BF16))
        copies.append(pltpu.make_async_copy(grads.at[tap], grad_hbm.at[tap], sems.at[tap]))
        copies[-1].start()
    for m in range(micro):
        cells = paths_ref[m]
        cells = pltpu.roll(cells, lax.rem(size - me, size) * span, 1)
        for r in range(rows):
            traj_ref[0, m, :, r, :] = cells[:chans, r * width:(r + 1) * width]
    for copy in copies:
        copy.wait()


def local(noise, target, timesteps, w_in, gn_gain, w_time1, w_time2, w_conv, w_out):
    size = lax.axis_size("tensor")
    micro, chans, rows, width = noise.shape
    features = w_in.shape[1]
    temb = w_time1.shape[1]
    taps = w_conv.shape[0]
    side = math.isqrt(taps)
    steps = timesteps.shape[0]
    height = rows * size
    lanes = height * width
    span = rows * width
    qrows = (1 + chans) * R
    tcols = taps * R
    block = -(-span // LANES) * LANES
    share = features // size
    vmem = pl.BlockSpec(memory_space=pltpu.VMEM)
    smem = pl.BlockSpec(memory_space=pltpu.SMEM)
    hbm = pl.BlockSpec(memory_space=pl.ANY)
    dma = pltpu.SemaphoreType.DMA
    wout_t = w_out.T
    paths, g = pl.pallas_call(
        functools.partial(chain_kernel, (height, width, features, steps, chans, side, size, micro)),
        out_shape=(jax.ShapeDtypeStruct((micro, R, lanes), F32), jax.ShapeDtypeStruct((tcols, features), F32)),
        in_specs=[smem, vmem, vmem, vmem, vmem, vmem, hbm, hbm, hbm],
        out_specs=(vmem, vmem),
        scratch_shapes=[
            pltpu.VMEM((features, temb), F32),
            pltpu.VMEM((features, temb), F32),
            pltpu.VMEM((taps, features, features), BF16),
            dma((3,)),
            pltpu.VMEM((micro, 2 * R, block), F32),
            pltpu.VMEM((size - 1, 2 * R, block), F32),
            dma((size - 1,)),
            dma((size - 1,)),
            pltpu.VMEM((steps + 1, R, lanes), F32),
            pltpu.VMEM((micro - 1, R, lanes), F32),
            pltpu.VMEM((tcols, features), F32),
            pltpu.VMEM((micro - 1, tcols, features), F32),
            dma((micro - 1, 2)),
            dma((micro - 1, 2)),
            pltpu.VMEM((steps, features, lanes), BF16),
            pltpu.VMEM((steps, features, lanes), F32),
            pltpu.VMEM((steps, features, LANES), F32),
            pltpu.VMEM((steps, features, LANES), F32),
            pltpu.VMEM((steps, features, LANES), F32),
            pltpu.VMEM((features + R, 6 * R), BF16),
            pltpu.VMEM((2 * features, 6 * qrows), BF16),
            pltpu.VMEM((2 * qrows, features), BF16),
            pltpu.VMEM((features + R, 3 * tcols), BF16),
            pltpu.VMEM((2 * tcols, features), BF16),
            pltpu.VMEM((4 * R, features), BF16),
            pltpu.VMEM((tcols, lanes), F32),
            pltpu.VMEM((steps, R, LANES), F32),
            pltpu.VMEM((2 * tcols, features), F32),
            pltpu.VMEM((steps, R, LANES), F32),
            pltpu.VMEM((steps, R, LANES), F32),
        ],
        compiler_params=pltpu.CompilerParams(vmem_limit_bytes=60 * 1024 * 1024, collective_id=0, has_side_effects=True),
        name="chain",
    )(timesteps, noise, target, w_in, gn_gain, wout_t, w_time1, w_time2.T, w_conv)
    trajectory, grad = pl.pallas_call(
        functools.partial(finish_kernel, (size, taps, span)),
        out_shape=(jax.ShapeDtypeStruct((1,) + noise.shape, F32), jax.ShapeDtypeStruct((taps, share, features), F32)),
        in_specs=[vmem, vmem, vmem],
        out_specs=(vmem, hbm),
        scratch_shapes=[pltpu.VMEM((taps, share, features), F32), dma((taps,))],
        name="finish",
    )(paths, g, wout_t)
    return trajectory, jnp.transpose(grad, (0, 2, 1))


def solution(mesh):
    placed = (P(None, None, "tensor", None), P(None, None, "tensor", None)) + (P(),) * 7
    return jax.shard_map(
        local,
        mesh=mesh,
        in_specs=placed,
        out_specs=(P("section", None, None, "tensor", None), P(None, None, "tensor")),
        check_vma=False,
    )
```

```python
import functools
import math

import jax
import jax.numpy as jnp
from jax import lax
from jax.experimental import pallas as pl
from jax.experimental.pallas import tpu as pltpu
from jax.sharding import PartitionSpec as P

GROUPS = 32
MESH = pl.DeviceIdType.MESH
HIGH = lax.Precision.HIGHEST
F32 = jnp.float32
BF16 = jnp.bfloat16
R = 8
LANES = 128
UNROLL_F = 8
UNROLL_B = 8


def parts3(x):
    high = x.astype(BF16).astype(F32)
    rest = x - high
    mid = rest.astype(BF16).astype(F32)
    low = (rest - mid).astype(BF16).astype(F32)
    return high, mid, low


def parts2(x):
    high = x.astype(BF16)
    return high, (x - high.astype(F32)).astype(BF16)


def iota(shape, axis):
    return lax.broadcasted_iota(jnp.int32, shape, axis)


def nn(a, b, precision=None):
    return lax.dot_general(a, b, (((1,), (0,)), ((), ())), precision=precision, preferred_element_type=F32)


def nt(a, b, precision=None):
    return lax.dot_general(a, b, (((1,), (1,)), ((), ())), precision=precision, preferred_element_type=F32)


def tn(a, b, precision=None):
    return lax.dot_general(a, b, (((0,), (0,)), ((), ())), precision=precision, preferred_element_type=F32)


def wide(column, lanes):
    return jnp.concatenate([column] * (lanes // LANES), axis=1) if lanes > LANES else column


def dot3(a, b, dot):
    ah, am = parts2(a)
    bh, bm = parts2(b)
    return dot(ah, bh) + dot(am, bh) + dot(ah, bm)


def everywhere(value, combine):
    for axis in (1, 0):
        step = value.shape[axis] // 2
        while step:
            value = combine(value, pltpu.roll(value, step, axis))
            step //= 2
    return value


def step_coefficients(ts_ref, steps, keep_s, noise_s):
    index = iota((R, LANES), 0) * LANES + iota((R, LANES), 1)
    lowest = jnp.sqrt(jnp.full((R, LANES), 0.00085, F32))
    highest = jnp.sqrt(jnp.full((R, LANES), 0.012, F32))
    betas = (lowest + index.astype(F32) * ((highest - lowest) / 999.0)) ** 2
    factors = 1.0 - betas
    bars = [everywhere(jnp.where(index <= ts_ref[s], factors, 1.0), jnp.multiply) for s in range(steps)]
    bars.append(jnp.ones((R, LANES), F32))
    for s in range(steps):
        keep = jnp.sqrt(bars[s + 1] / bars[s])
        keep_s[s] = keep
        noise_s[s] = jnp.sqrt(1.0 - bars[s + 1]) - keep * jnp.sqrt(1.0 - bars[s])


def sinusoid(ts_ref, steps, features):
    half = features // 2
    shape = (steps, features)
    row, lane = iota(shape, 0), iota(shape, 1)
    times = jnp.zeros(shape, jnp.int32)
    for s in range(steps):
        times = jnp.where(row == s, ts_ref[s], times)
    place = jnp.where(lane < half, lane, lane - half).astype(F32)
    angles = times.astype(F32) * jnp.exp(-math.log(10000.0) * place / half)
    return jnp.where(lane < half, jnp.cos(angles), jnp.sin(angles))


def chain_kernel(dims, ts_ref, noise_ref, target_ref, win_ref, gain_ref, wout_ref, w1_hbm, w2_hbm, wc_hbm,
                 paths_ref, g_ref, w1, w2, wc, sems, mine, slots, send, recv, path, arrived, gsend, garrived, send2, recv2,
                 act_s, z_s, scale_s, avg_s, rstd_s, wext, sm6, smt, v3, vt3, w2t, mask, ebs, gacc, keep_s, noise_s):
    height, width, features, steps, chans, taps_side, size, micro = dims
    taps = taps_side * taps_side
    lanes = height * width
    rows = height // size
    span = rows * width
    per_group = features // GROUPS
    count = float(lanes * per_group)
    blocks = 1 + chans
    qrows = blocks * R
    tcols = taps * R
    section = lax.axis_index("section")
    me = lax.axis_index("tensor")
    own = lax.rem(me, micro)

    barrier = pltpu.get_barrier_semaphore()
    peers = [lax.rem(me + d, size) for d in range(1, size)]
    for peer in peers:
        pl.semaphore_signal(barrier, inc=1, device_id={"tensor": peer}, device_id_type=MESH)
    copies = [pltpu.make_async_copy(src, dst, sems.at[i]) for i, (src, dst) in enumerate(((wc_hbm, wc), (w1_hbm, w1), (w2_hbm, w2)))]
    for copy in copies:
        copy.start()
    mine[...] = jnp.zeros_like(mine)
    for m in range(micro):
        for r in range(rows):
            mine[m, :chans, r * width:(r + 1) * width] = noise_ref[m, :, r, :]
            mine[m, R:R + chans, r * width:(r + 1) * width] = target_ref[m, :, r, :]
    step_coefficients(ts_ref, steps, keep_s, noise_s)
    sines = sinusoid(ts_ref, steps, features)

    lane = iota((1, lanes), 1)
    row, col = lane // width, lane % width
    offsets = []
    for tap in range(taps):
        dy, dx = tap // taps_side - taps_side // 2, tap % taps_side - taps_side // 2
        offsets.append(dy * width + dx)
        ok = (row + dy >= 0) & (row + dy < height) & (col + dx >= 0) & (col + dx < width)
        mask[tap * R:(tap + 1) * R] = jnp.broadcast_to(ok.astype(F32), (R, lanes))

    win, woutT = win_ref[...], wout_ref[...]
    if chans < R:
        fill = jnp.zeros((R - chans, features), F32)
        win, woutT = jnp.concatenate([win, fill], axis=0), jnp.concatenate([woutT, fill], axis=0)

    def tiled(weights, cols):
        high, mid, low = (part.astype(BF16) for part in parts3(weights))
        picker = (iota((R, cols), 1) % R == iota((R, cols), 0)).astype(BF16)
        return tn(high, picker) + tn(mid, picker) + tn(low, picker)

    win_t = tiled(win, 6 * qrows)
    wout_t = tiled(woutT, 3 * tcols)
    gain_row = gain_ref[...].reshape(1, features)
    gain_col = tn(gain_row, jnp.ones((1, LANES), F32), HIGH)

    pa, pb, pc = parts3(jnp.concatenate([win_t[:, :6 * R], dot3(woutT, win_t[:, :6 * R], nn)], axis=0))
    blk = iota((1, 6 * R), 1) // R
    wext[...] = jnp.where((blk == 2) | (blk == 4), pb, jnp.where(blk == 5, pc, pa)).astype(BF16)

    pl.semaphore_wait(barrier, size - 1)
    spread = [pltpu.make_async_remote_copy(
        src_ref=mine.at[lax.rem(peer, micro)], dst_ref=slots.at[d], send_sem=send.at[d], recv_sem=recv.at[d],
        device_id={"tensor": peer}, device_id_type=MESH) for d, peer in enumerate(peers)]
    for copy in spread:
        copy.start()

    qlane = iota((1, 6 * qrows), 1)
    qblk = (qlane % qrows) // R
    factor = jnp.ones_like(win_t)
    for c in range(chans):
        factor = jnp.where(qblk == c + 1, win_t[:, c:c + 1], factor)
    member = (iota((features, 1), 0) // per_group == iota((1, features), 1) // per_group).astype(BF16)
    sa, sb = parts2(win_t * factor)
    sums = (nn(member, sa) + nn(member, sb)) * (1.0 / count)
    sa, sb, sc = parts3(sums)
    rep = qlane // qrows
    chosen = jnp.where((rep == 2) | (rep == 4), sb, jnp.where(rep == 5, sc, sa))
    sm6[:features] = jnp.where(qblk == 0, chosen, 0.0).astype(BF16)
    sm6[features:] = jnp.where(qblk == 0, 0.0, chosen).astype(BF16)
    pad = -(-qrows // LANES) * LANES
    th, tm = parts2(jnp.transpose(sums[:, :pad])[:qrows])
    smt[:qrows] = th
    smt[qrows:] = tm
    wh, wm = parts2(jnp.concatenate([win, jnp.zeros((R, features), F32)], axis=0))
    w2t[:2 * R] = wh
    w2t[2 * R:] = wm

    tblk = iota((1, 3 * tcols), 1) // R % taps
    both = dot3(win, wout_t, nn)
    both = jnp.where(tblk == taps // 2, both, 0.0)
    oh, om = parts2(wout_t)
    copies[0].wait()
    v = jnp.zeros((features, 3 * tcols), F32)
    for start_tap in range(0, taps, taps_side):
        weights = wc[start_tap:start_tap + taps_side].reshape(taps_side * features, features)
        out = nn(weights, oh) + nn(weights, om)
        for i in range(taps_side):
            v = jnp.where(tblk == start_tap + i, out[i * features:(i + 1) * features], v)
    v_all = jnp.concatenate([v, both], axis=0)
    va, vb, _ = parts3(v_all)
    third = iota((1, 3 * tcols), 1) // tcols
    v3[...] = jnp.where(third == 1, vb, va).astype(BF16)
    cols = -(-2 * tcols // LANES) * LANES
    vT = jnp.transpose(v[:, :cols] if cols <= 3 * tcols else jnp.concatenate([v, jnp.zeros((features, cols - 3 * tcols), F32)], axis=1))[:2 * tcols]
    va, vb, _ = parts3(vT)
    vt3[...] = jnp.where(iota((2 * tcols, 1), 0) >= tcols, vb, va).astype(BF16)

    copies[1].wait()
    hh, hm = parts2(sines)
    stacked = jnp.concatenate([hh.astype(F32), hm.astype(F32)], axis=0).astype(BF16)
    wh, wm = parts2(w1[...])
    first = nn(stacked, wh)
    hidden = first[:steps] + first[steps:] + nn(stacked, wm)[:steps]
    hidden = hidden * (0.5 * jnp.tanh(0.5 * hidden) + 0.5)
    copies[2].wait()
    hh, hm = parts2(hidden)
    stacked = jnp.concatenate([hh.astype(F32), hm.astype(F32)], axis=0).astype(BF16)
    wh, wm = parts2(w2[...])
    first = nt(wh, stacked)
    embed = first[:, :steps] + first[:, steps:] + nt(wm, stacked)[:, :steps]
    embed_out = dot3(woutT, embed, nn)
    for s in range(steps):
        ebs[s] = jnp.broadcast_to(embed_out[:, s:s + 1], (R, LANES))

    def unrolled(block, owner):
        if lanes > block.shape[1]:
            block = jnp.concatenate([block, jnp.zeros((2 * R, lanes - block.shape[1]), F32)], axis=1)
        return pltpu.roll(block, owner * span, 1)

    both = unrolled(mine[own], me)
    for d, copy in enumerate(spread):
        copy.wait()
        both = both + unrolled(slots[d], lax.rem(me + size - 1 - d, size))
    start, target = both[:R], both[R:]

    def forward(s, x):
        xa, xb, xc = parts3(x)
        x6 = jnp.concatenate([xa, xb, xa, xc, xb, xa], axis=0).astype(BF16)
        projected = nn(wext[...], x6)
        q = jnp.concatenate([x] + [x * x[c:c + 1] for c in range(chans)], axis=0)
        qs = jnp.broadcast_to(jnp.sum(q, axis=1, keepdims=True), (qrows, LANES))
        qa, qb, qc = parts3(qs)
        q6 = jnp.concatenate([qa, qb, qa, qc, qb, qa], axis=0).astype(BF16)
        stats = nn(sm6[...], q6)
        average = stats[:features]
        variance = stats[features:] - average * average
        rstd = lax.rsqrt(variance + 1e-05)
        scale = rstd * gain_col
        avg_s[s] = average
        rstd_s[s] = rstd
        scale_s[s] = scale
        z = (projected[:features] - wide(average, lanes)) * wide(scale, lanes)
        z_s[s] = z
        act = (z * (0.5 * jnp.tanh(0.5 * z) + 0.5)).astype(BF16)
        act_s[s] = act
        y = nn(vt3[...], act)
        y = y[:tcols] + y[tcols:]
        guess = projected[features:] + wide(ebs[s], lanes)
        for tap in range(taps):
            piece = y[tap * R:(tap + 1) * R]
            if offsets[tap] % lanes:
                piece = pltpu.roll(piece, (-offsets[tap]) % lanes, 1) * mask[tap * R:(tap + 1) * R]
            guess = guess + piece
        x = wide(keep_s[s], lanes) * x + wide(noise_s[s], lanes) * guess
        path[s + 1] = x
        return x

    path[0] = start
    last = lax.fori_loop(0, steps, forward, start, unroll=min(steps, UNROLL_F))
    gacc[...] = jnp.zeros_like(gacc)

    def backward(i, adjoint):
        s = steps - 1 - i
        a = wide(noise_s[s], lanes) * adjoint
        shifted = []
        for tap in range(taps):
            piece = a
            if offsets[tap] % lanes:
                piece = pltpu.roll(a * mask[tap * R:(tap + 1) * R], offsets[tap] % lanes, 1)
            shifted.append(piece)
        shifted = jnp.concatenate(shifted, axis=0)
        high = shifted.astype(BF16).astype(F32)
        low = shifted - high
        a3 = jnp.concatenate([high, high, low], axis=0).astype(BF16)
        grads = nn(v3[...], a3)
        gacc[...] += nt(jnp.concatenate([high, low], axis=0).astype(BF16), act_s[s])
        z = z_s[s]
        sig = 0.5 * jnp.tanh(0.5 * z) + 0.5
        slope = sig + z * sig * (1.0 - sig)
        dz = grads[:features] * slope
        dzs = dz * wide(scale_s[s], lanes)
        rstd = rstd_s[s]
        e1 = jnp.broadcast_to(jnp.sum(dzs, axis=1, keepdims=True), (features, LANES))
        e2 = jnp.broadcast_to(jnp.sum(dz * z, axis=1, keepdims=True), (features, LANES)) * (rstd * rstd)
        pair = jnp.concatenate([e2 * avg_s[s] - e1, e2], axis=1)
        ph, pm = parts2(pair)
        k = nn(smt[...], ph)
        k = k[:qrows] + k[qrows:] + nn(smt[:qrows], pm)
        dh, dm = parts2(dzs)
        direct = nn(w2t[...], dh)
        direct = direct[:R] + direct[2 * R:3 * R] + nn(w2t[:2 * R], dm)[:R]
        result = wide(keep_s[s], lanes) * adjoint + grads[features:] + direct + wide(k[:R, :LANES], lanes)
        x = path[s]
        for c in range(chans):
            result = result - wide(k[(c + 1) * R:(c + 2) * R, LANES:], lanes) * x[c:c + 1]
        return result

    lax.fori_loop(0, steps, backward, last - target, unroll=min(steps, UNROLL_B))
    per = R // chans
    for tile in range(gsend.shape[0] // R):
        packed = jnp.zeros((R, features), F32)
        for i, tap in enumerate(range(tile * per, min(taps, (tile + 1) * per))):
            block = gacc[tap * R:(tap + 1) * R] + gacc[tcols + tap * R:tcols + (tap + 1) * R]
            packed = packed + (pltpu.roll(block, i * chans, 0) if i else block)
        gsend[tile * R:(tile + 1) * R] = packed
    partners = [me - own + lax.rem(own + d, micro) for d in range(1, micro)]
    swaps = []
    for d, partner in enumerate(partners):
        for k, (src, dst) in enumerate(((path.at[section + 1], arrived.at[d]), (gsend, garrived.at[d]))):
            swaps.append(pltpu.make_async_remote_copy(
                src_ref=src, dst_ref=dst, send_sem=send2.at[d, k], recv_sem=recv2.at[d, k],
                device_id={"tensor": partner}, device_id_type=MESH))
    for copy in swaps:
        copy.start()
    paths_ref[own] = path[section + 1]
    for copy in swaps:
        copy.wait()
    total = gsend[...]
    for d in range(micro - 1):
        total = total + garrived[d]
        paths_ref[lax.rem(own + micro - 1 - d, micro)] = arrived[d]
    g_ref[...] = total


def finish_kernel(dims, paths_ref, g_ref, wout_ref, traj_ref, grad_hbm, grads, sems):
    size, taps, span = dims
    me = lax.axis_index("tensor")
    _, micro, chans, rows, width = traj_ref.shape
    share = grads.shape[1]
    features = g_ref.shape[1]
    padded = -(-features // LANES) * LANES
    weights = jnp.concatenate([wout_ref[...], jnp.zeros((chans, padded - features), F32)], axis=1)
    weights = pltpu.roll(weights, lax.rem(padded - me * share, padded), 1)[:, :share]
    weights = jnp.concatenate([weights, jnp.zeros((R - chans, share), F32)], axis=0) if chans < R else weights
    per = R // chans
    lefts = []
    for i in range(per):
        wa, wb, _ = parts3(pltpu.roll(weights, i * chans, 0) if i else weights)
        lefts.append(jnp.concatenate([wa, wb, wa, wb], axis=0).astype(BF16))
    copies = []
    for tap in range(taps):
        if tap % per == 0:
            ga, gb, _ = parts3(g_ref[tap // per * R:(tap // per + 1) * R])
            right = jnp.concatenate([ga, ga, gb, gb], axis=0).astype(BF16)
        grads[tap] = tn(lefts[tap % per], right)
        copies.append(pltpu.make_async_copy(grads.at[tap], grad_hbm.at[tap], sems.at[tap]))
        copies[-1].start()
    for m in range(micro):
        cells = paths_ref[m]
        cells = pltpu.roll(cells, lax.rem(size - me, size) * span, 1)
        for r in range(rows):
            traj_ref[0, m, :, r, :] = cells[:chans, r * width:(r + 1) * width]
    for copy in copies:
        copy.wait()


def local(noise, target, timesteps, w_in, gn_gain, w_time1, w_time2, w_conv, w_out):
    size = lax.axis_size("tensor")
    micro, chans, rows, width = noise.shape
    features = w_in.shape[1]
    temb = w_time1.shape[1]
    taps = w_conv.shape[0]
    side = math.isqrt(taps)
    steps = timesteps.shape[0]
    height = rows * size
    lanes = height * width
    span = rows * width
    qrows = (1 + chans) * R
    tcols = taps * R
    grows = -(-taps // (R // chans)) * R
    block = -(-span // LANES) * LANES
    share = features // size
    vmem = pl.BlockSpec(memory_space=pltpu.VMEM)
    smem = pl.BlockSpec(memory_space=pltpu.SMEM)
    hbm = pl.BlockSpec(memory_space=pl.ANY)
    dma = pltpu.SemaphoreType.DMA
    wout_t = w_out.T
    paths, g = pl.pallas_call(
        functools.partial(chain_kernel, (height, width, features, steps, chans, side, size, micro)),
        out_shape=(pltpu.VMEM((micro, R, lanes), F32), pltpu.VMEM((grows, features), F32)),
        in_specs=[smem, vmem, vmem, vmem, vmem, vmem, hbm, hbm, hbm],
        out_specs=(vmem, vmem),
        scratch_shapes=[
            pltpu.VMEM((features, temb), F32),
            pltpu.VMEM((features, temb), F32),
            pltpu.VMEM((taps, features, features), BF16),
            dma((3,)),
            pltpu.VMEM((micro, 2 * R, block), F32),
            pltpu.VMEM((size - 1, 2 * R, block), F32),
            dma((size - 1,)),
            dma((size - 1,)),
            pltpu.VMEM((steps + 1, R, lanes), F32),
            pltpu.VMEM((micro - 1, R, lanes), F32),
            pltpu.VMEM((grows, features), F32),
            pltpu.VMEM((micro - 1, grows, features), F32),
            dma((micro - 1, 2)),
            dma((micro - 1, 2)),
            pltpu.VMEM((steps, features, lanes), BF16),
            pltpu.VMEM((steps, features, lanes), F32),
            pltpu.VMEM((steps, features, LANES), F32),
            pltpu.VMEM((steps, features, LANES), F32),
            pltpu.VMEM((steps, features, LANES), F32),
            pltpu.VMEM((features + R, 6 * R), BF16),
            pltpu.VMEM((2 * features, 6 * qrows), BF16),
            pltpu.VMEM((2 * qrows, features), BF16),
            pltpu.VMEM((features + R, 3 * tcols), BF16),
            pltpu.VMEM((2 * tcols, features), BF16),
            pltpu.VMEM((4 * R, features), BF16),
            pltpu.VMEM((tcols, lanes), F32),
            pltpu.VMEM((steps, R, LANES), F32),
            pltpu.VMEM((2 * tcols, features), F32),
            pltpu.VMEM((steps, R, LANES), F32),
            pltpu.VMEM((steps, R, LANES), F32),
        ],
        compiler_params=pltpu.CompilerParams(vmem_limit_bytes=60 * 1024 * 1024, collective_id=0, has_side_effects=True),
        name="chain",
    )(timesteps, noise, target, w_in, gn_gain, wout_t, w_time1, w_time2.T, w_conv)
    paths, g = (pltpu.with_memory_space_constraint(held, pltpu.VMEM) for held in (paths, g))
    trajectory, grad = pl.pallas_call(
        functools.partial(finish_kernel, (size, taps, span)),
        out_shape=(jax.ShapeDtypeStruct((1,) + noise.shape, F32), jax.ShapeDtypeStruct((taps, share, features), F32)),
        in_specs=[vmem, vmem, vmem],
        out_specs=(vmem, hbm),
        scratch_shapes=[pltpu.VMEM((taps, share, features), F32), dma((taps,))],
        name="finish",
    )(paths, g, wout_t)
    return trajectory, jnp.transpose(grad, (0, 2, 1))


def solution(mesh):
    placed = (P(None, None, "tensor", None), P(None, None, "tensor", None)) + (P(),) * 7
    return jax.shard_map(
        local,
        mesh=mesh,
        in_specs=placed,
        out_specs=(P("section", None, None, "tensor", None), P(None, None, "tensor")),
        check_vma=False,
    )
```

```python
import functools
import math

import jax
import jax.numpy as jnp
from jax import lax
from jax.experimental import pallas as pl
from jax.experimental.pallas import tpu as pltpu
from jax.sharding import PartitionSpec as P

GROUPS = 32
MESH = pl.DeviceIdType.MESH
HIGH = lax.Precision.HIGHEST
F32 = jnp.float32
BF16 = jnp.bfloat16
R = 8
LANES = 128
UNROLL_F = 8
UNROLL_B = 8


def parts3(x):
    high = x.astype(BF16).astype(F32)
    rest = x - high
    mid = rest.astype(BF16).astype(F32)
    low = (rest - mid).astype(BF16).astype(F32)
    return high, mid, low


def parts2(x):
    high = x.astype(BF16)
    return high, (x - high.astype(F32)).astype(BF16)


def iota(shape, axis):
    return lax.broadcasted_iota(jnp.int32, shape, axis)


def nn(a, b, precision=None):
    return lax.dot_general(a, b, (((1,), (0,)), ((), ())), precision=precision, preferred_element_type=F32)


def nt(a, b, precision=None):
    return lax.dot_general(a, b, (((1,), (1,)), ((), ())), precision=precision, preferred_element_type=F32)


def tn(a, b, precision=None):
    return lax.dot_general(a, b, (((0,), (0,)), ((), ())), precision=precision, preferred_element_type=F32)


def wide(column, lanes):
    return jnp.concatenate([column] * (lanes // LANES), axis=1) if lanes > LANES else column


def dot3(a, b, dot):
    ah, am = parts2(a)
    bh, bm = parts2(b)
    return dot(ah, bh) + dot(am, bh) + dot(ah, bm)


def everywhere(value, combine):
    for axis in (1, 0):
        step = value.shape[axis] // 2
        while step:
            value = combine(value, pltpu.roll(value, step, axis))
            step //= 2
    return value


def step_coefficients(ts_ref, steps, keep_s, noise_s):
    index = iota((R, LANES), 0) * LANES + iota((R, LANES), 1)
    lowest = jnp.sqrt(jnp.full((R, LANES), 0.00085, F32))
    highest = jnp.sqrt(jnp.full((R, LANES), 0.012, F32))
    betas = (lowest + index.astype(F32) * ((highest - lowest) / 999.0)) ** 2
    factors = 1.0 - betas
    bars = [everywhere(jnp.where(index <= ts_ref[s], factors, 1.0), jnp.multiply) for s in range(steps)]
    bars.append(jnp.ones((R, LANES), F32))
    for s in range(steps):
        keep = jnp.sqrt(bars[s + 1] / bars[s])
        keep_s[s] = keep
        noise_s[s] = jnp.sqrt(1.0 - bars[s + 1]) - keep * jnp.sqrt(1.0 - bars[s])


def sinusoid(ts_ref, steps, features):
    half = features // 2
    shape = (steps, features)
    row, lane = iota(shape, 0), iota(shape, 1)
    times = jnp.zeros(shape, jnp.int32)
    for s in range(steps):
        times = jnp.where(row == s, ts_ref[s], times)
    place = jnp.where(lane < half, lane, lane - half).astype(F32)
    angles = times.astype(F32) * jnp.exp(-math.log(10000.0) * place / half)
    return jnp.where(lane < half, jnp.cos(angles), jnp.sin(angles))


def chain_kernel(dims, ts_ref, noise_ref, target_ref, win_ref, gain_ref, wout_ref, w1_hbm, w2_hbm, wc_hbm,
                 paths_ref, g_ref, wout_kept, w1, w2, wc, sems, mine, slots, send, recv, path, arrived, gsend, garrived, send2, recv2,
                 act_s, z_s, scale_s, avg_s, rstd_s, wext, sm6, smt, v3, vt3, w2t, mask, ebs, gacc, keep_s, noise_s):
    height, width, features, steps, chans, taps_side, size, micro = dims
    taps = taps_side * taps_side
    lanes = height * width
    rows = height // size
    span = rows * width
    per_group = features // GROUPS
    count = float(lanes * per_group)
    blocks = 1 + chans
    qrows = blocks * R
    tcols = taps * R
    section = lax.axis_index("section")
    me = lax.axis_index("tensor")
    own = lax.rem(me, micro)

    barrier = pltpu.get_barrier_semaphore()
    peers = [lax.rem(me + d, size) for d in range(1, size)]
    for peer in peers:
        pl.semaphore_signal(barrier, inc=1, device_id={"tensor": peer}, device_id_type=MESH)
    copies = [pltpu.make_async_copy(src, dst, sems.at[i]) for i, (src, dst) in enumerate(((wc_hbm, wc), (w1_hbm, w1), (w2_hbm, w2)))]
    for copy in copies:
        copy.start()
    mine[...] = jnp.zeros_like(mine)
    for m in range(micro):
        for r in range(rows):
            mine[m, :chans, r * width:(r + 1) * width] = noise_ref[m, :, r, :]
            mine[m, R:R + chans, r * width:(r + 1) * width] = target_ref[m, :, r, :]
    step_coefficients(ts_ref, steps, keep_s, noise_s)
    sines = sinusoid(ts_ref, steps, features)

    lane = iota((1, lanes), 1)
    row, col = lane // width, lane % width
    offsets = []
    for tap in range(taps):
        dy, dx = tap // taps_side - taps_side // 2, tap % taps_side - taps_side // 2
        offsets.append(dy * width + dx)
        ok = (row + dy >= 0) & (row + dy < height) & (col + dx >= 0) & (col + dx < width)
        mask[tap * R:(tap + 1) * R] = jnp.broadcast_to(ok.astype(F32), (R, lanes))

    win, woutT = win_ref[...], wout_ref[...]
    if chans < R:
        fill = jnp.zeros((R - chans, features), F32)
        win, woutT = jnp.concatenate([win, fill], axis=0), jnp.concatenate([woutT, fill], axis=0)

    def tiled(weights, cols):
        high, mid, low = (part.astype(BF16) for part in parts3(weights))
        picker = (iota((R, cols), 1) % R == iota((R, cols), 0)).astype(BF16)
        return tn(high, picker) + tn(mid, picker) + tn(low, picker)

    wout_kept[...] = woutT
    win_t = tiled(win, 6 * qrows)
    wout_t = tiled(woutT, 3 * tcols)
    gain_row = gain_ref[...].reshape(1, features)
    gain_col = tn(gain_row, jnp.ones((1, LANES), F32), HIGH)

    pa, pb, pc = parts3(jnp.concatenate([win_t[:, :6 * R], dot3(woutT, win_t[:, :6 * R], nn)], axis=0))
    blk = iota((1, 6 * R), 1) // R
    wext[...] = jnp.where((blk == 2) | (blk == 4), pb, jnp.where(blk == 5, pc, pa)).astype(BF16)

    pl.semaphore_wait(barrier, size - 1)
    spread = [pltpu.make_async_remote_copy(
        src_ref=mine.at[lax.rem(peer, micro)], dst_ref=slots.at[d], send_sem=send.at[d], recv_sem=recv.at[d],
        device_id={"tensor": peer}, device_id_type=MESH) for d, peer in enumerate(peers)]
    for copy in spread:
        copy.start()

    qlane = iota((1, 6 * qrows), 1)
    qblk = (qlane % qrows) // R
    factor = jnp.ones_like(win_t)
    for c in range(chans):
        factor = jnp.where(qblk == c + 1, win_t[:, c:c + 1], factor)
    member = (iota((features, 1), 0) // per_group == iota((1, features), 1) // per_group).astype(BF16)
    sa, sb = parts2(win_t * factor)
    sums = (nn(member, sa) + nn(member, sb)) * (1.0 / count)
    sa, sb, sc = parts3(sums)
    rep = qlane // qrows
    chosen = jnp.where((rep == 2) | (rep == 4), sb, jnp.where(rep == 5, sc, sa))
    sm6[:features] = jnp.where(qblk == 0, chosen, 0.0).astype(BF16)
    sm6[features:] = jnp.where(qblk == 0, 0.0, chosen).astype(BF16)
    pad = -(-qrows // LANES) * LANES
    th, tm = parts2(jnp.transpose(sums[:, :pad])[:qrows])
    smt[:qrows] = th
    smt[qrows:] = tm
    wh, wm = parts2(jnp.concatenate([win, jnp.zeros((R, features), F32)], axis=0))
    w2t[:2 * R] = wh
    w2t[2 * R:] = wm

    tblk = iota((1, 3 * tcols), 1) // R % taps
    both = dot3(win, wout_t, nn)
    both = jnp.where(tblk == taps // 2, both, 0.0)
    oh, om = parts2(wout_t[:, :LANES])
    halves = jnp.where(iota((1, LANES), 1) // R % 2 == 0, oh.astype(F32), om.astype(F32)).astype(BF16)
    copies[0].wait()
    v = jnp.zeros((features, 3 * tcols), F32)
    for start_tap in range(0, taps, taps_side):
        weights = wc[start_tap:start_tap + taps_side].reshape(taps_side * features, features)
        out = nn(weights, halves)
        out = out + pltpu.roll(out, R, 1)
        out = jnp.concatenate([out] * (-(-3 * tcols // LANES)), axis=1)[:, :3 * tcols]
        for i in range(taps_side):
            v = jnp.where(tblk == start_tap + i, out[i * features:(i + 1) * features], v)
    v_all = jnp.concatenate([v, both], axis=0)
    va, vb, _ = parts3(v_all)
    third = iota((1, 3 * tcols), 1) // tcols
    v3[...] = jnp.where(third == 1, vb, va).astype(BF16)
    cols = -(-2 * tcols // LANES) * LANES
    vT = jnp.transpose(v[:, :cols] if cols <= 3 * tcols else jnp.concatenate([v, jnp.zeros((features, cols - 3 * tcols), F32)], axis=1))[:2 * tcols]
    va, vb, _ = parts3(vT)
    vt3[...] = jnp.where(iota((2 * tcols, 1), 0) >= tcols, vb, va).astype(BF16)

    copies[1].wait()
    hh, hm = parts2(sines)
    stacked = jnp.concatenate([hh.astype(F32), hm.astype(F32)], axis=0).astype(BF16)
    wh, wm = parts2(w1[...])
    first = nn(stacked, wh)
    hidden = first[:steps] + first[steps:] + nn(stacked, wm)[:steps]
    hidden = hidden * (0.5 * jnp.tanh(0.5 * hidden) + 0.5)
    copies[2].wait()
    hh, hm = parts2(hidden)
    stacked = jnp.concatenate([hh.astype(F32), hm.astype(F32)], axis=0).astype(BF16)
    wh, wm = parts2(w2[...])
    first = nt(wh, stacked)
    embed = first[:, :steps] + first[:, steps:] + nt(wm, stacked)[:, :steps]
    embed_out = dot3(woutT, embed, nn)
    for s in range(steps):
        ebs[s] = jnp.broadcast_to(embed_out[:, s:s + 1], (R, LANES))

    def unrolled(block, owner):
        if lanes > block.shape[1]:
            block = jnp.concatenate([block, jnp.zeros((2 * R, lanes - block.shape[1]), F32)], axis=1)
        return pltpu.roll(block, owner * span, 1)

    both = unrolled(mine[own], me)
    for d, copy in enumerate(spread):
        copy.wait()
        both = both + unrolled(slots[d], lax.rem(me + size - 1 - d, size))
    start, target = both[:R], both[R:]

    def forward(s, x):
        xa, xb, xc = parts3(x)
        x6 = jnp.concatenate([xa, xb, xa, xc, xb, xa], axis=0).astype(BF16)
        projected = nn(wext[...], x6)
        q = jnp.concatenate([x] + [x * x[c:c + 1] for c in range(chans)], axis=0)
        qs = jnp.broadcast_to(jnp.sum(q, axis=1, keepdims=True), (qrows, LANES))
        qa, qb, qc = parts3(qs)
        q6 = jnp.concatenate([qa, qb, qa, qc, qb, qa], axis=0).astype(BF16)
        stats = nn(sm6[...], q6)
        average = stats[:features]
        variance = stats[features:] - average * average
        rstd = lax.rsqrt(variance + 1e-05)
        scale = rstd * gain_col
        avg_s[s] = average
        rstd_s[s] = rstd
        scale_s[s] = scale
        z = (projected[:features] - wide(average, lanes)) * wide(scale, lanes)
        z_s[s] = z
        act = (z * (0.5 * jnp.tanh(0.5 * z) + 0.5)).astype(BF16)
        act_s[s] = act
        y = nn(vt3[...], act)
        y = y[:tcols] + y[tcols:]
        guess = projected[features:] + wide(ebs[s], lanes)
        for tap in range(taps):
            piece = y[tap * R:(tap + 1) * R]
            if offsets[tap] % lanes:
                piece = pltpu.roll(piece, (-offsets[tap]) % lanes, 1) * mask[tap * R:(tap + 1) * R]
            guess = guess + piece
        x = wide(keep_s[s], lanes) * x + wide(noise_s[s], lanes) * guess
        path[s + 1] = x
        return x

    path[0] = start
    last = lax.fori_loop(0, steps, forward, start, unroll=min(steps, UNROLL_F))
    gacc[...] = jnp.zeros_like(gacc)

    def backward(i, adjoint):
        s = steps - 1 - i
        a = wide(noise_s[s], lanes) * adjoint
        shifted = []
        for tap in range(taps):
            piece = a
            if offsets[tap] % lanes:
                piece = pltpu.roll(a * mask[tap * R:(tap + 1) * R], offsets[tap] % lanes, 1)
            shifted.append(piece)
        shifted = jnp.concatenate(shifted, axis=0)
        high = shifted.astype(BF16).astype(F32)
        low = shifted - high
        a3 = jnp.concatenate([high, high, low], axis=0).astype(BF16)
        grads = nn(v3[...], a3)
        gacc[...] += nt(jnp.concatenate([high, low], axis=0).astype(BF16), act_s[s])
        z = z_s[s]
        sig = 0.5 * jnp.tanh(0.5 * z) + 0.5
        slope = sig + z * sig * (1.0 - sig)
        dz = grads[:features] * slope
        dzs = dz * wide(scale_s[s], lanes)
        rstd = rstd_s[s]
        e1 = jnp.broadcast_to(jnp.sum(dzs, axis=1, keepdims=True), (features, LANES))
        e2 = jnp.broadcast_to(jnp.sum(dz * z, axis=1, keepdims=True), (features, LANES)) * (rstd * rstd)
        pair = jnp.concatenate([e2 * avg_s[s] - e1, e2], axis=1)
        ph, pm = parts2(pair)
        k = nn(smt[...], ph)
        k = k[:qrows] + k[qrows:] + nn(smt[:qrows], pm)
        dh, dm = parts2(dzs)
        direct = nn(w2t[...], dh)
        direct = direct[:R] + direct[2 * R:3 * R] + nn(w2t[:2 * R], dm)[:R]
        result = wide(keep_s[s], lanes) * adjoint + grads[features:] + direct + wide(k[:R, :LANES], lanes)
        x = path[s]
        for c in range(chans):
            result = result - wide(k[(c + 1) * R:(c + 2) * R, LANES:], lanes) * x[c:c + 1]
        return result

    lax.fori_loop(0, steps, backward, last - target, unroll=min(steps, UNROLL_B))
    per = R // chans
    for tile in range(gsend.shape[0] // R):
        packed = jnp.zeros((R, features), F32)
        for i, tap in enumerate(range(tile * per, min(taps, (tile + 1) * per))):
            block = gacc[tap * R:(tap + 1) * R] + gacc[tcols + tap * R:tcols + (tap + 1) * R]
            packed = packed + (pltpu.roll(block, i * chans, 0) if i else block)
        gsend[tile * R:(tile + 1) * R] = packed
    partners = [me - own + lax.rem(own + d, micro) for d in range(1, micro)]
    swaps = []
    for d, partner in enumerate(partners):
        for k, (src, dst) in enumerate(((path.at[section + 1], arrived.at[d]), (gsend, garrived.at[d]))):
            swaps.append(pltpu.make_async_remote_copy(
                src_ref=src, dst_ref=dst, send_sem=send2.at[d, k], recv_sem=recv2.at[d, k],
                device_id={"tensor": partner}, device_id_type=MESH))
    for copy in swaps:
        copy.start()
    paths_ref[own] = path[section + 1]
    for copy in swaps:
        copy.wait()
    total = gsend[...]
    for d in range(micro - 1):
        total = total + garrived[d]
        paths_ref[lax.rem(own + micro - 1 - d, micro)] = arrived[d]
    g_ref[...] = total


def finish_kernel(dims, paths_ref, g_ref, wout_ref, traj_ref, grad_hbm, grads, traj, sems):
    size, taps, span = dims
    me = lax.axis_index("tensor")
    _, micro, chans, rows, width = traj_ref.shape
    share = grads.shape[1]
    features = g_ref.shape[1]
    padded = -(-features // LANES) * LANES
    weights = jnp.concatenate([wout_ref[...], jnp.zeros((R, padded - features), F32)], axis=1)
    weights = pltpu.roll(weights, lax.rem(padded - me * share, padded), 1)[:, :share]
    per = R // chans
    lefts = []
    for i in range(per):
        wa, wb, _ = parts3(pltpu.roll(weights, i * chans, 0) if i else weights)
        lefts.append(jnp.concatenate([wa, wb, wa, wb], axis=0).astype(BF16))
    for m in range(micro):
        cells = paths_ref[m]
        cells = pltpu.roll(cells, lax.rem(size - me, size) * span, 1)
        for r in range(rows):
            traj[0, m, :, r, :] = cells[:chans, r * width:(r + 1) * width]
    copies = [pltpu.make_async_copy(traj, traj_ref, sems.at[taps])]
    copies[0].start()
    for tap in range(taps):
        if tap % per == 0:
            ga, gb, _ = parts3(g_ref[tap // per * R:(tap // per + 1) * R])
            right = jnp.concatenate([ga, ga, gb, gb], axis=0).astype(BF16)
        grads[tap] = tn(lefts[tap % per], right)
        copies.append(pltpu.make_async_copy(grads.at[tap], grad_hbm.at[tap], sems.at[tap]))
        copies[-1].start()
    for copy in copies:
        copy.wait()


def local(noise, target, timesteps, w_in, gn_gain, w_time1, w_time2, w_conv, w_out):
    size = lax.axis_size("tensor")
    micro, chans, rows, width = noise.shape
    features = w_in.shape[1]
    temb = w_time1.shape[1]
    taps = w_conv.shape[0]
    side = math.isqrt(taps)
    steps = timesteps.shape[0]
    height = rows * size
    lanes = height * width
    span = rows * width
    qrows = (1 + chans) * R
    tcols = taps * R
    grows = -(-taps // (R // chans)) * R
    block = -(-span // LANES) * LANES
    share = features // size
    vmem = pl.BlockSpec(memory_space=pltpu.VMEM)
    smem = pl.BlockSpec(memory_space=pltpu.SMEM)
    hbm = pl.BlockSpec(memory_space=pl.ANY)
    dma = pltpu.SemaphoreType.DMA
    wout_t = w_out.T
    held = pl.pallas_call(
        functools.partial(chain_kernel, (height, width, features, steps, chans, side, size, micro)),
        out_shape=(pltpu.VMEM((micro, R, lanes), F32), pltpu.VMEM((grows, features), F32), pltpu.VMEM((R, features), F32)),
        in_specs=[smem, vmem, vmem, vmem, vmem, vmem, hbm, hbm, hbm],
        out_specs=(vmem, vmem, vmem),
        scratch_shapes=[
            pltpu.VMEM((features, temb), F32),
            pltpu.VMEM((features, temb), F32),
            pltpu.VMEM((taps, features, features), BF16),
            dma((3,)),
            pltpu.VMEM((micro, 2 * R, block), F32),
            pltpu.VMEM((size - 1, 2 * R, block), F32),
            dma((size - 1,)),
            dma((size - 1,)),
            pltpu.VMEM((steps + 1, R, lanes), F32),
            pltpu.VMEM((micro - 1, R, lanes), F32),
            pltpu.VMEM((grows, features), F32),
            pltpu.VMEM((micro - 1, grows, features), F32),
            dma((micro - 1, 2)),
            dma((micro - 1, 2)),
            pltpu.VMEM((steps, features, lanes), BF16),
            pltpu.VMEM((steps, features, lanes), F32),
            pltpu.VMEM((steps, features, LANES), F32),
            pltpu.VMEM((steps, features, LANES), F32),
            pltpu.VMEM((steps, features, LANES), F32),
            pltpu.VMEM((features + R, 6 * R), BF16),
            pltpu.VMEM((2 * features, 6 * qrows), BF16),
            pltpu.VMEM((2 * qrows, features), BF16),
            pltpu.VMEM((features + R, 3 * tcols), BF16),
            pltpu.VMEM((2 * tcols, features), BF16),
            pltpu.VMEM((4 * R, features), BF16),
            pltpu.VMEM((tcols, lanes), F32),
            pltpu.VMEM((steps, R, LANES), F32),
            pltpu.VMEM((2 * tcols, features), F32),
            pltpu.VMEM((steps, R, LANES), F32),
            pltpu.VMEM((steps, R, LANES), F32),
        ],
        compiler_params=pltpu.CompilerParams(vmem_limit_bytes=60 * 1024 * 1024, collective_id=0, has_side_effects=True),
        name="chain",
    )(timesteps, noise, target, w_in, gn_gain, wout_t, w_time1, w_time2.T, w_conv)
    held = [pltpu.with_memory_space_constraint(one, pltpu.VMEM) for one in held]
    trajectory, grad = pl.pallas_call(
        functools.partial(finish_kernel, (size, taps, span)),
        out_shape=(jax.ShapeDtypeStruct((1,) + noise.shape, F32), jax.ShapeDtypeStruct((taps, share, features), F32)),
        in_specs=[vmem, vmem, vmem],
        out_specs=(hbm, hbm),
        scratch_shapes=[pltpu.VMEM((taps, share, features), F32), pltpu.VMEM((1,) + noise.shape, F32), dma((taps + 1,))],
        name="finish",
    )(*held)
    return trajectory, jnp.transpose(grad, (0, 2, 1))


def solution(mesh):
    placed = (P(None, None, "tensor", None), P(None, None, "tensor", None)) + (P(),) * 7
    return jax.shard_map(
        local,
        mesh=mesh,
        in_specs=placed,
        out_specs=(P("section", None, None, "tensor", None), P(None, None, "tensor")),
        check_vma=False,
    )
```
